512 devices in a mesh: pipe: 16 (over z), expert: 32 (over x, y, core).
Axes of the slice: x: 4, y: 4, z: 16, core: 2. Of those that a mesh axis runs over, the one named last changes fastest.
Arguments:
- state: bfloat16 [16, 256, 7168], P('pipe', 'expert'), may hold values from -6 to 6
- fresh: bfloat16 [1, 256, 7168], P(None, 'expert'), may hold values from -6 to 6
- gain: bfloat16 [16, 7168], P('pipe'), may hold values from 0.099609375 to 1.8984375
- w_up: bfloat16 [16, 7168, 4096], P('pipe', None, 'expert'), may hold values from -0.0625 to 0.0625
- w_down: bfloat16 [16, 4096, 7168], P('pipe', 'expert'), may hold values from -0.1875 to 0.1875
- route_ids: int32 [2, 16, 256, 2], P(None, 'pipe', 'expert'), may hold values from 0 to 3, all different within a row; in each aligned block of 8 rows (0 to 7, 8 to 15, ..., all dimensions but the last counted through in order) at most 8 rows name the same one
- gates: float32 [2, 16, 256, 2], P(None, 'pipe', 'expert'), may hold values from 0.05 to 0.5
Outputs:
- after: bfloat16 [16, 256, 7168], P('pipe', 'expert')
The draws below stay inside these ranges and needn't reach their ends.
Inputs may be any that keep to these rules, and one draw needn't show every extreme that they name: `route_ids`: each token names 2 different experts. Among the 8 tokens of one device at one step and section (aligned blocks of 8 tokens) no expert is named more than 8 times, a bound that some block reaches.
All inputs are finite; a program needn't handle non-finite values.
Results may differ from the reference program's by a relative error of at most 0.006.
Values may be sent and summed in bfloat16 or wider, within the bound.
No kernel may reach another device: no remote copies, remote signals or barrier semaphores. Data moves between devices by JAX's collectives and lax.ppermute only.
A program may use at most 64 MiB of HBM per device.

```python
import math
import jax
import jax.numpy as jnp
import numpy as np
from jax import lax

D = 7168
H = 1024
TOPK = 2
EXPERTS = 4
TOK_DEV = 8
TICKS = 2
SECTIONS = 16
GROUP = 8
HS = 128
CAP = 8
TOKENS = 256
N_EXPERT = 32


def block_scale(rng, extent, split, smallest, high):
    level = 1.0
    for dim, parts in split:
        draws = jax.random.uniform(jax.random.fold_in(jax.random.fold_in(rng, 6), dim), (parts,), jnp.float32, smallest / len(split), high / len(split))
        level = level * jnp.repeat(jnp.exp(draws), extent[dim] // parts).reshape((-1,) + (1,) * (len(extent) - 1 - dim))
    return level


def routed_block(key, own, number, rows, count, top, bound, slope):
    sequence = jax.random.permutation(key, count)
    crowded, usual = shares(count, rows * top, bound, slope, True), shares(count, rows * top, bound, slope, False)
    places = jnp.arange(count)

    def named(tallies, rotation):
        used = int((tallies > 0).sum())
        fixed = max(1, used // 4)
        moved = fixed + (places - fixed + rotation * (used - fixed)) % max(1, count - fixed)
        return jnp.zeros((count,), jnp.int32).at[sequence[jnp.where(places < fixed, places, moved)]].set(jnp.asarray(tallies, jnp.int32))

    tallies = jnp.where(number % 4 == 0, named(crowded, number // 4), named(usual, number - number // 4 - 1))
    mixed = jax.random.permutation(jax.random.fold_in(own, 3), count)
    donor, taker = mixed[0:count // 2 * 2:2], mixed[1:count // 2 * 2:2]
    room = jnp.minimum(tallies[donor] - 1, bound - tallies[taker]) // 2
    room = jnp.where((donor == sequence[0]) | (taker == sequence[0]) | (tallies[taker] == 0), 0, jnp.maximum(room, 0))
    moved = jax.random.randint(jax.random.fold_in(own, 4), (count // 2,), 0, 1 << 20) % (room + 1)
    tallies = tallies.at[donor].add(-moved).at[taker].add(moved)
    labels = jnp.searchsorted(jnp.cumsum(tallies), jnp.arange(rows * top), side="right").astype(jnp.int32)
    table = labels.reshape(top, rows).T
    table = table[jax.random.permutation(jax.random.fold_in(own, 1), rows)]
    rotation = jax.random.randint(jax.random.fold_in(own, 2), (rows, 1), 0, top)
    return jnp.take_along_axis(table, (jnp.arange(top)[None, :] + rotation) % top, axis=1)


def shares(amount, total, reach, skew, full):
    portions = [(1 << 20) // math.isqrt(grade ** skew) + 1 for grade in range(1, amount + 1)]
    largest = reach if full else min(reach, max(-(-total // amount), total * portions[0] // sum(portions)))
    least = 1 if total - largest >= amount - 1 else 0
    given, rest = [largest] + [least] * (amount - 1), total - largest - least * (amount - 1)
    while rest > 0:
        movable = [i for i in range(1, amount) if given[i] < largest] or [i for i in range(1, amount) if given[i] < reach]
        mass, remaining = sum([portions[i] for i in movable]), rest
        for i in movable:
            extra = min(reach - given[i], max(1, remaining * portions[i] // mass), rest)
            given[i] = given[i] + extra
            rest = rest - extra
    return np.array(given)


def scatter_about(key, extent, deviation, limit, split=(), held_as=jnp.bfloat16):
    result = deviation * jax.random.normal(key, extent, jnp.float32)
    if split:
        result = result * block_scale(key, extent, split, -0.22, 0.18)
    return jnp.clip(result, -limit, limit).astype(held_as)


def setup_inputs(seed: int = 0) -> dict:
    seeds = jax.random.split(jax.random.key(seed), 8)
    state = scatter_about(seeds[0], (SECTIONS, TOKENS, D), 1.0, 6.0, ((0, 16), (1, 32)))
    fresh = scatter_about(seeds[1], (TICKS - 1, TOKENS, D), 1.0, 6.0, ((1, 32),))
    gain = jnp.clip(1.0 + 0.18 * jax.random.normal(seeds[2], (SECTIONS, D), jnp.float32), 0.099609375, 1.8984375).astype(jnp.bfloat16)
    w_up = scatter_about(seeds[3], (SECTIONS, D, EXPERTS * H), D ** -0.5, 0.0625, ((0, 16), (2, 32)))
    w_down = scatter_about(seeds[4], (SECTIONS, EXPERTS * H, D), H ** -0.5, 0.1875, ((0, 16), (1, 32)))
    route_ids_keys = jax.random.split(jax.random.fold_in(seeds[5], 1), TICKS * SECTIONS * TOKENS // TOK_DEV)
    route_ids_turns = jax.random.permutation(jax.random.fold_in(seeds[5], 3), TICKS * SECTIONS * TOKENS // TOK_DEV)
    route_ids = jax.vmap(lambda own, number: routed_block(jax.random.fold_in(seeds[5], 2), own, number, TOK_DEV, EXPERTS, TOPK, CAP, 2))(route_ids_keys, route_ids_turns).reshape((TICKS, SECTIONS, TOKENS, TOPK))
    gates = jnp.clip(jnp.exp(math.log(0.5) - 2.3025851 * jax.random.uniform(seeds[6], (TICKS, SECTIONS, TOKENS, TOPK), jnp.float32) ** block_scale(seeds[6], (TICKS, SECTIONS, TOKENS, TOPK), ((1, 16), (2, 32)), -0.2, 0.2)), 0.05, 0.5)
    return dict(state=state, fresh=fresh, gain=gain, w_up=w_up, w_down=w_down, route_ids=route_ids, gates=gates)


def rms_scaled(rows_in, gain_row):
    wide = rows_in.astype(jnp.float32)
    square = lax.optimization_barrier(jnp.mean(wide * wide, axis=-1, keepdims=True))
    return (wide * lax.rsqrt(square + 1e-06) * gain_row.astype(jnp.float32)).astype(jnp.bfloat16)

def slot_numbers(blocks, experts):
    onehot = (blocks[..., None] == jnp.arange(experts, dtype=jnp.int32)).astype(jnp.int32)
    before = jnp.cumsum(onehot, axis=-2) - onehot
    return lax.optimization_barrier(jnp.sum(before * onehot, axis=-1)).astype(jnp.int32)

def expert_apply(rows_in, weight_up, weight_down):
    hidden = jax.nn.silu(jnp.dot(rows_in, weight_up, preferred_element_type=jnp.float32)).astype(jnp.bfloat16)
    count = hidden.shape[0]
    pieces = jnp.einsum('rgh,ghd->grd', hidden.reshape(count, GROUP, HS).astype(jnp.float32), weight_down.reshape(GROUP, HS, D).astype(jnp.float32))
    return lax.optimization_barrier(jnp.sum(pieces.astype(jnp.bfloat16).astype(jnp.float32), axis=0))

def moe_layer(current, gain_row, section_up, section_down, chosen, gate_rows):
    normed = rms_scaled(current, gain_row)
    weight_up = section_up.reshape(D, EXPERTS, H).transpose(1, 0, 2)
    weight_down = section_down.reshape(EXPERTS, H, D)
    slot_ids = slot_numbers(chosen.reshape(N_EXPERT, TOK_DEV * TOPK), EXPERTS).reshape(TOKENS, TOPK)
    source = (jnp.arange(TOKENS, dtype=jnp.int32) // TOK_DEV)[:, None]
    position = ((chosen * N_EXPERT + source) * CAP + slot_ids).reshape(-1).astype(jnp.int32)
    buffer = jnp.zeros((EXPERTS * N_EXPERT * CAP, D), normed.dtype).at[position].set(jnp.repeat(normed, TOPK, axis=0))
    outputs = lax.map(lambda members: expert_apply(*members), (buffer.reshape(EXPERTS, N_EXPERT * CAP, D), weight_up, weight_down))
    picked = outputs.reshape(-1, D)[position].reshape(TOKENS, TOPK, D)
    mixed = current.astype(jnp.float32) + lax.optimization_barrier(jnp.sum(gate_rows[..., None].astype(jnp.float32) * picked, axis=1))
    return mixed.astype(jnp.bfloat16)

def reference(state, fresh, gain, w_up, w_down, route_ids, gates):
    current = state
    outputs = state
    for step_index in range(TICKS):
        outputs = lax.map(lambda members: moe_layer(*members), (current, gain, w_up, w_down, route_ids[step_index], gates[step_index]))
        if step_index < TICKS - 1:
            current = jnp.concatenate([fresh[step_index][None], outputs[:-1]], axis=0)
    return outputs
```

```python
import jax
import jax.numpy as jnp
from jax import lax
from jax.experimental import pallas as pl
from jax.experimental.pallas import tpu as pltpu
from jax.sharding import Mesh, PartitionSpec as P

EXPERTS = 4
TICKS = 2
CORES = 2
STAGGER = 15000
TILE = 1024
VMEM = pl.BlockSpec(memory_space=pltpu.VMEM)


def shifted(block, axis, distance):
    devices = range(lax.axis_size(axis))
    route = [(i - distance, i) for i in devices if i - distance in devices]
    return lax.ppermute(block, axis, route)


def swapped(block):
    return lax.ppermute(block, "core", [(i, CORES - 1 - i) for i in range(CORES)])


def rms_scaled(rows_in, gain_row):
    wide = rows_in.astype(jnp.float32)
    square = jnp.mean(wide * wide, axis=-1, keepdims=True)
    return (wide * lax.rsqrt(square + 1e-06) * gain_row.astype(jnp.float32)).astype(jnp.bfloat16)


def exchanged(blocks):
    return lax.all_to_all(blocks, ("plane", "line"), split_axis=0, concat_axis=0, tiled=True)


def first_normed(rows_in, gain_rows, peers):
    def kernel(rows_ref, gain_ref, out_ref):
        normed = rms_scaled(rows_ref[...], gain_ref[...])
        for i in range(peers):
            out_ref[i] = normed

        @pl.when(lax.axis_index("core") != 0)
        def _():
            pl.delay(STAGGER)

    return pl.pallas_call(
        kernel,
        out_shape=jax.ShapeDtypeStruct((peers, *rows_in.shape), jnp.bfloat16),
        in_specs=[VMEM, VMEM],
        out_specs=VMEM,
        compiler_params=pltpu.CompilerParams(vmem_limit_bytes=8 << 20),
    )(rows_in, gain_rows)


def expert_apply(rows_in, up_own, up_other, down_own, down_other):
    count, width = rows_in.shape
    tiles = width // TILE

    def kernel(rows_ref, up_a, up_b, down_a, down_b, out_ref, made, sems):
        def tile(i):
            return pl.ds(i * TILE, TILE)

        raised = 0.0
        for i in range(tiles):
            units = jnp.concatenate([up_a[tile(i), :], up_b[tile(i), :]], axis=1)
            raised = raised + jnp.dot(
                rows_ref[:, tile(i)], units, preferred_element_type=jnp.float32
            )
        hidden = (raised / (1.0 + jnp.exp(-raised))).astype(jnp.bfloat16)
        copies = []
        for i in range(tiles):
            units = jnp.concatenate([down_a[:, tile(i)], down_b[:, tile(i)]], axis=0)
            made[:, tile(i)] = jnp.dot(
                hidden, units, preferred_element_type=jnp.float32
            ).astype(jnp.bfloat16)
            copy = pltpu.make_async_copy(made.at[:, tile(i)], out_ref.at[:, tile(i)], sems.at[i])
            copy.start()
            copies.append(copy)
        for copy in copies:
            copy.wait()

    return pl.pallas_call(
        kernel,
        out_shape=jax.ShapeDtypeStruct((count, width), jnp.bfloat16),
        in_specs=[VMEM] * 5,
        out_specs=pl.BlockSpec(memory_space=pl.ANY),
        scratch_shapes=[
            pltpu.VMEM((count, width), jnp.bfloat16),
            pltpu.SemaphoreType.DMA((tiles,)),
        ],
        compiler_params=pltpu.CompilerParams(vmem_limit_bytes=16 << 20),
        cost_estimate=pl.CostEstimate(
            flops=8 * count * width * up_own.shape[1],
            transcendentals=2 * count * up_own.shape[1],
            bytes_accessed=2 * width * (2 * count + 4 * up_own.shape[1]),
        ),
    )(rows_in, up_own, up_other, down_own, down_other)


def body(state, fresh, gain, w_up, w_down, route_ids, gates):
    lines = lax.axis_size("line")
    peers = lax.axis_size("plane") * lines
    rows = state.shape[1]
    width = state.shape[2]
    section_index = lax.axis_index("pipe")
    weights = (w_up[0], swapped(w_up[0]), w_down[0], swapped(w_down[0]))
    current = state[0]
    for step_index in range(TICKS):
        if step_index == 0:
            sent = first_normed(current, gain, peers)
        else:
            normed = rms_scaled(current, gain[0])
            sent = jnp.broadcast_to(normed[None], (peers, rows, width))
        received = exchanged(sent)
        partial_value = expert_apply(received.reshape(peers * rows, width), *weights)
        returned = exchanged(partial_value.reshape(peers, rows, width))
        chosen = route_ids[step_index, 0][..., None] == jnp.arange(EXPERTS, dtype=jnp.int32)
        weight = jnp.sum(jnp.where(chosen, gates[step_index, 0][..., None], 0.0), axis=1)
        summed = jnp.sum(returned.reshape(EXPERTS, lines, rows, width).astype(jnp.float32), axis=1)
        expert_sum = jnp.sum(weight.T[..., None] * summed, axis=0)
        produced = (current.astype(jnp.float32) + expert_sum).astype(jnp.bfloat16)
        if step_index < TICKS - 1:
            arrived = shifted(produced, "pipe", 1)
            current = jnp.where(section_index == 0, fresh[step_index], arrived)
    return produced[None]


def solution(mesh):
    sections, devices = mesh.devices.shape
    lines = devices // (EXPERTS * CORES)
    grid = Mesh(
        mesh.devices.reshape(sections, EXPERTS, lines, CORES), ("pipe", "plane", "line", "core")
    )
    expert = ("plane", "line", "core")
    placed = (
        P("pipe", expert, None),
        P(None, expert, None),
        P("pipe", None),
        P("pipe", None, expert),
        P("pipe", expert, None),
        P(None, "pipe", expert, None),
        P(None, "pipe", expert, None),
    )
    return jax.shard_map(
        body, mesh=grid, in_specs=placed, out_specs=P("pipe", expert, None), check_vma=False
    )
```

```python
import jax
import jax.numpy as jnp
from jax import lax
from jax.experimental import pallas as pl
from jax.experimental.pallas import tpu as pltpu
from jax.sharding import Mesh, PartitionSpec as P

EXPERTS = 4
TICKS = 2
CORES = 2
EXPERT_AXES = ("plane", "line", "core")
STAGGER = 12500
TILE = 1024
VMEM = pl.BlockSpec(memory_space=pltpu.VMEM)


def shifted(block, axis, distance):
    devices = range(lax.axis_size(axis))
    route = [(i - distance, i) for i in devices if i - distance in devices]
    return lax.ppermute(block, axis, route)


def swapped(block):
    return lax.ppermute(block, "core", [(i, CORES - 1 - i) for i in range(CORES)])


def rms_scaled(rows_in, gain_row):
    wide = rows_in.astype(jnp.float32)
    square = jnp.mean(wide * wide, axis=-1, keepdims=True)
    return (wide * lax.rsqrt(square + 1e-06) * gain_row.astype(jnp.float32)).astype(jnp.bfloat16)


def leader(plane, line):
    return (plane + line) % CORES


def exchanged(blocks):
    lines = lax.axis_size("line")
    chips = [(plane, line) for plane in range(lax.axis_size("plane")) for line in range(lines)]
    groups = [
        [(plane * lines + line) * CORES + (leader(plane, line) + turn) % CORES for plane, line in chips]
        for turn in range(CORES)
    ]
    return lax.all_to_all(
        blocks, EXPERT_AXES, split_axis=0, concat_axis=0, axis_index_groups=groups, tiled=True
    )


def first_normed(rows_in, gain_rows, peers):
    def kernel(rows_hbm, gain_hbm, out_ref, rows_ref, gain_ref, sems):
        copies = [
            pltpu.make_async_copy(rows_hbm, rows_ref, sems.at[0]),
            pltpu.make_async_copy(gain_hbm, gain_ref, sems.at[1]),
        ]
        for copy in copies:
            copy.start()
        for copy in copies:
            copy.wait()
        normed = rms_scaled(rows_ref[...], gain_ref[...])
        for i in range(peers):
            out_ref[i] = normed

        @pl.when(lax.axis_index("core") != leader(lax.axis_index("plane"), lax.axis_index("line")))
        def _():
            pl.delay(STAGGER)

    return pl.pallas_call(
        kernel,
        out_shape=jax.ShapeDtypeStruct((peers, *rows_in.shape), jnp.bfloat16),
        in_specs=[pl.BlockSpec(memory_space=pl.ANY)] * 2,
        out_specs=VMEM,
        scratch_shapes=[
            pltpu.VMEM(rows_in.shape, jnp.bfloat16),
            pltpu.VMEM(gain_rows.shape, jnp.bfloat16),
            pltpu.SemaphoreType.DMA((2,)),
        ],
        compiler_params=pltpu.CompilerParams(vmem_limit_bytes=8 << 20),
    )(rows_in, gain_rows)


def expert_apply(rows_in, up_own, up_other, down_own, down_other):
    count, width = rows_in.shape
    tiles = width // TILE

    def kernel(rows_ref, up_a, up_b, down_a, down_b, out_ref):
        def tile(i):
            return pl.ds(i * TILE, TILE)

        raised = 0.0
        for i in range(tiles):
            units = jnp.concatenate([up_a[tile(i), :], up_b[tile(i), :]], axis=1)
            raised = raised + jnp.dot(
                rows_ref[:, tile(i)], units, preferred_element_type=jnp.float32
            )
        hidden = (raised / (1.0 + jnp.exp(-raised))).astype(jnp.bfloat16)
        for i in range(tiles):
            units = jnp.concatenate([down_a[:, tile(i)], down_b[:, tile(i)]], axis=0)
            out_ref[:, tile(i)] = jnp.dot(
                hidden, units, preferred_element_type=jnp.float32
            ).astype(jnp.bfloat16)

    return pl.pallas_call(
        kernel,
        out_shape=jax.ShapeDtypeStruct((count, width), jnp.bfloat16),
        in_specs=[VMEM] * 5,
        out_specs=VMEM,
        compiler_params=pltpu.CompilerParams(vmem_limit_bytes=16 << 20),
        cost_estimate=pl.CostEstimate(
            flops=8 * count * width * up_own.shape[1],
            transcendentals=2 * count * up_own.shape[1],
            bytes_accessed=2 * width * (2 * count + 4 * up_own.shape[1]),
        ),
    )(rows_in, up_own, up_other, down_own, down_other)


def body(state, fresh, gain, w_up, w_down, route_ids, gates):
    lines = lax.axis_size("line")
    peers = lax.axis_size("plane") * lines
    rows = state.shape[1]
    width = state.shape[2]
    section_index = lax.axis_index("pipe")
    weights = (w_up[0], swapped(w_up[0]), w_down[0], swapped(w_down[0]))
    chosen = route_ids[:, 0, ..., None] == jnp.arange(EXPERTS, dtype=jnp.int32)
    weights_home = jnp.sum(jnp.where(chosen, gates[:, 0, ..., None], 0.0), axis=2)
    weights_home = [weights_home[step_index].T for step_index in range(TICKS)]
    current = state[0]
    for step_index in range(TICKS):
        if step_index == 0:
            sent = first_normed(current, gain, peers)
            sent, weights_home = lax.optimization_barrier((sent, weights_home))
        else:
            normed = rms_scaled(current, gain[0])
            sent = jnp.broadcast_to(normed[None], (peers, rows, width))
        received = exchanged(sent)
        partial_value = expert_apply(received.reshape(peers * rows, width), *weights)
        returned = exchanged(partial_value.reshape(peers, rows, width))
        summed = jnp.sum(returned.reshape(EXPERTS, lines, rows, width).astype(jnp.float32), axis=1)
        expert_sum = jnp.sum(weights_home[step_index][..., None] * summed, axis=0)
        produced = (current.astype(jnp.float32) + expert_sum).astype(jnp.bfloat16)
        if step_index < TICKS - 1:
            arrived = shifted(produced, "pipe", 1)
            current = jnp.where(section_index == 0, fresh[step_index], arrived)
    return produced[None]


def solution(mesh):
    sections, devices = mesh.devices.shape
    lines = devices // (EXPERTS * CORES)
    grid = Mesh(
        mesh.devices.reshape(sections, EXPERTS, lines, CORES), ("pipe", *EXPERT_AXES)
    )
    placed = (
        P("pipe", EXPERT_AXES, None),
        P(None, EXPERT_AXES, None),
        P("pipe", None),
        P("pipe", None, EXPERT_AXES),
        P("pipe", EXPERT_AXES, None),
        P(None, "pipe", EXPERT_AXES, None),
        P(None, "pipe", EXPERT_AXES, None),
    )
    return jax.shard_map(
        body, mesh=grid, in_specs=placed, out_specs=P("pipe", EXPERT_AXES, None), check_vma=False
    )
```

```python
import jax
import jax.numpy as jnp
from jax import lax
from jax.experimental import pallas as pl
from jax.experimental.pallas import tpu as pltpu
from jax.sharding import Mesh, PartitionSpec as P

EXPERTS = 4
TICKS = 2
CORES = 2
EXPERT_AXES = ("plane", "line", "core")
STAGGER = 12500
TILE = 1024
VMEM = pl.BlockSpec(memory_space=pltpu.VMEM)


def shifted(block, axis, distance):
    devices = range(lax.axis_size(axis))
    route = [(i - distance, i) for i in devices if i - distance in devices]
    return lax.ppermute(block, axis, route)


def swapped(block):
    return lax.ppermute(block, "core", [(i, CORES - 1 - i) for i in range(CORES)])


def rms_scaled(rows_in, gain_row):
    wide = rows_in.astype(jnp.float32)
    square = jnp.mean(wide * wide, axis=-1, keepdims=True)
    return (wide * lax.rsqrt(square + 1e-06) * gain_row.astype(jnp.float32)).astype(jnp.bfloat16)


def leader(plane, line):
    return (plane + line) % CORES


def exchanged(blocks):
    lines = lax.axis_size("line")
    chips = [(plane, line) for plane in range(lax.axis_size("plane")) for line in range(lines)]
    groups = [
        [(plane * lines + line) * CORES + (leader(plane, line) + turn) % CORES for plane, line in chips]
        for turn in range(CORES)
    ]
    return lax.all_to_all(
        blocks, EXPERT_AXES, split_axis=0, concat_axis=0, axis_index_groups=groups, tiled=True
    )


def opening(rows_in, gain_rows, ids, values, peers):
    def kernel(rows_hbm, gain_hbm, ids_hbm, values_hbm, sent_ref, kept_ref, *refs):
        homes, held, sems = refs[:TICKS], refs[TICKS:-1], refs[-1]
        sources = (rows_hbm, gain_hbm, ids_hbm, values_hbm)
        copies = [
            pltpu.make_async_copy(source, target, sems.at[i])
            for i, (source, target) in enumerate(zip(sources, held))
        ]
        for copy in copies:
            copy.start()
        for copy in copies:
            copy.wait()
        rows_ref, gain_ref, ids_ref, values_ref = held
        normed = rms_scaled(rows_ref[...], gain_ref[...])
        kept_ref[...] = rows_ref[...]
        for i in range(peers):
            sent_ref[i] = normed
        for step_index, home_ref in enumerate(homes):
            number = lax.broadcasted_iota(jnp.int32, home_ref.shape, 0)
            total = jnp.zeros(home_ref.shape, jnp.float32)
            for k in range(ids_ref.shape[1]):
                named = ids_ref[step_index, k : k + 1, :] == number
                total = total + jnp.where(named, values_ref[step_index, k : k + 1, :], 0.0)
            home_ref[...] = total

        @pl.when(lax.axis_index("core") != leader(lax.axis_index("plane"), lax.axis_index("line")))
        def _():
            pl.delay(STAGGER)

    operands = [
        pltpu.with_memory_space_constraint(each, pltpu.HBM)
        for each in (rows_in, gain_rows, ids, values)
    ]
    sent = jax.ShapeDtypeStruct((peers, *rows_in.shape), jnp.bfloat16)
    kept = jax.ShapeDtypeStruct(rows_in.shape, jnp.bfloat16)
    home = jax.ShapeDtypeStruct((EXPERTS, rows_in.shape[0]), jnp.float32)
    return pl.pallas_call(
        kernel,
        out_shape=[sent, kept] + [home] * TICKS,
        in_specs=[pl.BlockSpec(memory_space=pl.ANY)] * len(operands),
        out_specs=[VMEM] * (2 + TICKS),
        scratch_shapes=[pltpu.VMEM(each.shape, each.dtype) for each in (rows_in, gain_rows, ids, values)]
        + [pltpu.SemaphoreType.DMA((len(operands),))],
        compiler_params=pltpu.CompilerParams(vmem_limit_bytes=8 << 20),
    )(*operands)


def expert_apply(rows_in, up_own, up_other, down_own, down_other):
    count, width = rows_in.shape
    tiles = width // TILE

    def kernel(rows_ref, up_a, up_b, down_a, down_b, out_ref):
        def tile(i):
            return pl.ds(i * TILE, TILE)

        raised = 0.0
        for i in range(tiles):
            units = jnp.concatenate([up_a[tile(i), :], up_b[tile(i), :]], axis=1)
            raised = raised + jnp.dot(
                rows_ref[:, tile(i)], units, preferred_element_type=jnp.float32
            )
        hidden = (raised / (1.0 + jnp.exp(-raised))).astype(jnp.bfloat16)
        for i in range(tiles):
            units = jnp.concatenate([down_a[:, tile(i)], down_b[:, tile(i)]], axis=0)
            out_ref[:, tile(i)] = jnp.dot(
                hidden, units, preferred_element_type=jnp.float32
            ).astype(jnp.bfloat16)

    return pl.pallas_call(
        kernel,
        out_shape=jax.ShapeDtypeStruct((count, width), jnp.bfloat16),
        in_specs=[VMEM] * 5,
        out_specs=VMEM,
        compiler_params=pltpu.CompilerParams(vmem_limit_bytes=16 << 20),
        cost_estimate=pl.CostEstimate(
            flops=8 * count * width * up_own.shape[1],
            transcendentals=2 * count * up_own.shape[1],
            bytes_accessed=2 * width * (2 * count + 4 * up_own.shape[1]),
        ),
    )(rows_in, up_own, up_other, down_own, down_other)


def body(state, fresh, gain, w_up, w_down, route_ids, gates):
    lines = lax.axis_size("line")
    peers = lax.axis_size("plane") * lines
    rows = state.shape[1]
    width = state.shape[2]
    section_index = lax.axis_index("pipe")
    weights = (w_up[0], swapped(w_up[0]), w_down[0], swapped(w_down[0]))
    ids, values = (each[:, 0].transpose(0, 2, 1) for each in (route_ids, gates))
    current = state[0]
    for step_index in range(TICKS):
        if step_index == 0:
            sent, current, *weights_home = opening(current, gain, ids, values, peers)
        else:
            normed = rms_scaled(current, gain[0])
            sent = jnp.broadcast_to(normed[None], (peers, rows, width))
        received = exchanged(sent)
        partial_value = expert_apply(received.reshape(peers * rows, width), *weights)
        returned = exchanged(partial_value.reshape(peers, rows, width))
        summed = jnp.sum(returned.reshape(EXPERTS, lines, rows, width).astype(jnp.float32), axis=1)
        expert_sum = jnp.sum(weights_home[step_index][..., None] * summed, axis=0)
        produced = (current.astype(jnp.float32) + expert_sum).astype(jnp.bfloat16)
        if step_index < TICKS - 1:
            arrived = shifted(produced, "pipe", 1)
            current = jnp.where(section_index == 0, fresh[step_index], arrived)
    return produced[None]


def solution(mesh):
    sections, devices = mesh.devices.shape
    lines = devices // (EXPERTS * CORES)
    grid = Mesh(
        mesh.devices.reshape(sections, EXPERTS, lines, CORES), ("pipe", *EXPERT_AXES)
    )
    placed = (
        P("pipe", EXPERT_AXES, None),
        P(None, EXPERT_AXES, None),
        P("pipe", None),
        P("pipe", None, EXPERT_AXES),
        P("pipe", EXPERT_AXES, None),
        P(None, "pipe", EXPERT_AXES, None),
        P(None, "pipe", EXPERT_AXES, None),
    )
    return jax.shard_map(
        body, mesh=grid, in_specs=placed, out_specs=P("pipe", EXPERT_AXES, None), check_vma=False
    )
```
